256 devices in a mesh: pts: 128 (over y, x, z_lo, core), grp: 2 (over z_hi).
Axes of the slice: x: 4, y: 4, z: 8 (z_hi: 2, z_lo: 4; z = z_hi * 4 + z_lo), core: 2. Of those that a mesh axis runs over, the one named last changes fastest.
Arguments:
- grid_states: float32 [59, 2097152], P(None, ('pts', 'grp')), may hold values from 0 to 1
- coarse_active: int32 [16384, 8], P(('pts', 'grp')), may hold values from 0 to 127, all different within a row
- fine_active: int32 [16384, 8], P(('pts', 'grp')), may hold values from 0 to 31, all different within a row
- shock: int32 [2097152], P(('pts', 'grp')), may hold values from 0 to 3
- coarse_surplus: bfloat16 [4, 60, 16384], P(None, 'grp', 'pts'), may hold values from -0.796875 to 0.796875
- fine_surplus: bfloat16 [4, 60, 524288], P(None, 'grp', 'pts'), may hold values from -0.796875 to 0.796875
- coarse_dim: int32 [128], P('pts'), may hold values from 0 to 58
- coarse_level: int32 [128], P('pts'), may hold values from 0 to 2
- fine_dim: int32 [4096], P('pts'), may hold values from 0 to 58
- fine_level: int32 [4096], P('pts'), may hold values from 0 to 2
- tfp: float32 [4], replicated, may hold values from 0.5 to 2
- trans_weight: float32 [4, 4], replicated, may hold values from 0.2 to 5
Outputs:
- savings: bfloat16 [4, 60, 2097152], P(None, None, ('pts', 'grp'))
- prices: float32 [2, 2097152], P(None, ('pts', 'grp'))
The draws below stay inside these ranges and needn't reach their ends.
Inputs may be any that keep to these rules, and one draw needn't show every extreme that they name: `coarse_active`: each row names 8 different coarse blocks, and every coarse block is named by some row. `fine_active`: each row names 8 different fine blocks of its region.
All inputs are finite; a program needn't handle non-finite values.
Results may differ from the reference program's by a relative error of at most 0.0034.
Values may be sent and summed in bfloat16 or wider, within the bound.
A program may use at most 128 MiB of HBM per device.

```python
import math
import jax
import jax.numpy as jnp
from jax import lax

S = 4
GEN = 60
NSTATE = 59
BS = 128
NCOARSE = 128
NF = 32
KC = 8
KF = 8
TILE = 128
NFINE = 4096
POINTS = 2097152
TILES = 16384
N_PTS = 128


def plant(drawn, rng, least, top_value):
    longest = drawn.shape.index(max(drawn.shape))
    spots = []
    for shift in (0, 1):
        where = [jax.random.randint(jax.random.fold_in(rng, axis), (), 0, length) for axis, length in enumerate(drawn.shape)]
        where[longest] = (where[longest] + shift) % drawn.shape[longest]
        spots.append(tuple(where))
    return drawn.at[spots[0]].set(least).at[spots[1]].set(top_value)


def block_levels(rng, extent, split, least, largest):
    factor_of, own = 1.0, jax.random.fold_in(rng, 6)
    for dim, parts in split:
        steps = jnp.exp(jax.random.uniform(jax.random.fold_in(own, dim), (parts,), jnp.float32, least / len(split), largest / len(split)))
        factor_of = factor_of * jnp.repeat(steps, extent[dim] // parts).reshape([-1 if axis == dim else 1 for axis in range(len(extent))])
    return factor_of


def distinct(key, rows, number_of, top, lift):
    ranking = jax.random.permutation(jax.random.fold_in(key, 1), number_of)
    favour = ranking
    for power in range(3):
        favour = favour * favour // number_of
    favour = favour * lift // number_of
    chance = jax.random.randint(jax.random.fold_in(key, 2), (rows, number_of), 0, 4096) + favour
    fixed_rows = jax.random.permutation(jax.random.fold_in(key, 3), rows)[jnp.arange(number_of) % rows]
    chance = jnp.where(jnp.arange(rows)[:, None] == fixed_rows[None, :], 1 << 14, chance)
    merit = chance * number_of + jnp.arange(number_of)
    return lax.top_k(merit.astype(jnp.int32), top)[1].astype(jnp.int32)


def gaussian(own_key, shape, deviation, reach, pieces=(), held_as=jnp.bfloat16):
    factor_of = block_levels(own_key, shape, pieces, -0.22, 0.18) if pieces else 1.0
    entries = jax.random.normal(own_key, shape, jnp.float32) * deviation * factor_of
    return jnp.minimum(jnp.maximum(entries, -reach), reach).astype(held_as)


def setup_inputs(seed: int = 0) -> dict:
    arg_keys = jax.random.split(jax.random.key(seed), 13)
    grid_states = jnp.clip(1.0 * jax.random.uniform(arg_keys[0], (NSTATE, POINTS), jnp.float32) ** block_levels(arg_keys[0], (NSTATE, POINTS), ((1, 256),), -0.2, 0.2), 0.0, 1.0)
    coarse_active = distinct(arg_keys[1], TILES, NCOARSE, KC, 512)
    fine_active = distinct(arg_keys[2], TILES, NF, KF, 2048)
    shock = plant(jax.random.randint(arg_keys[3], (POINTS,), 0, S), jax.random.fold_in(arg_keys[3], 1), 0, S - 1).astype(jnp.int32)
    coarse_surplus = gaussian(arg_keys[4], (S, GEN, NCOARSE * BS), 0.2, 0.796875, ((1, 2), (2, 128)))
    fine_surplus = gaussian(arg_keys[5], (S, GEN, NFINE * BS), 0.2, 0.796875, ((1, 2), (2, 128)))
    coarse_dim = plant(jax.random.randint(arg_keys[6], (NCOARSE,), 0, NSTATE), jax.random.fold_in(arg_keys[6], 1), 0, NSTATE - 1).astype(jnp.int32)
    coarse_level = plant(jax.random.randint(arg_keys[7], (NCOARSE,), 0, 3), jax.random.fold_in(arg_keys[7], 1), 0, 2).astype(jnp.int32)
    fine_dim = plant(jax.random.randint(arg_keys[8], (NFINE,), 0, NSTATE), jax.random.fold_in(arg_keys[8], 1), 0, NSTATE - 1).astype(jnp.int32)
    fine_level = plant(jax.random.randint(arg_keys[9], (NFINE,), 0, 3), jax.random.fold_in(arg_keys[9], 1), 0, 2).astype(jnp.int32)
    tfp = jnp.clip(jnp.exp(jax.random.uniform(arg_keys[10], (S,), jnp.float32, math.log(0.5), math.log(2.0))), 0.5, 2.0)
    trans_weight = jnp.clip(jnp.exp(jax.random.uniform(arg_keys[11], (S, S), jnp.float32, math.log(0.2), math.log(5.0))), 0.2, 5.0)
    return dict(grid_states=grid_states, coarse_active=coarse_active, fine_active=fine_active, shock=shock, coarse_surplus=coarse_surplus, fine_surplus=fine_surplus, coarse_dim=coarse_dim, coarse_level=coarse_level, fine_dim=fine_dim, fine_level=fine_level, tfp=tfp, trans_weight=trans_weight)


def reference(grid_states, coarse_active, fine_active, shock, coarse_surplus, fine_surplus, coarse_dim, coarse_level, fine_dim, fine_level, tfp, trans_weight):
    table = jnp.concatenate([coarse_surplus.reshape(S * GEN, NCOARSE * BS), fine_surplus.reshape(S * GEN, NFINE * BS)], axis=1)
    region = (jnp.arange(TILES, dtype=jnp.int32) // (TILES // N_PTS)).astype(jnp.int32)
    block_ids = jnp.concatenate([coarse_active.astype(jnp.int32), (NCOARSE + region[:, None] * NF + fine_active).astype(jnp.int32)], axis=1)
    block_dim = jnp.concatenate([coarse_dim, fine_dim]).astype(jnp.int32)
    block_level = jnp.concatenate([coarse_level, fine_level]).astype(jnp.int32)
    states_tiles = grid_states.reshape(NSTATE, TILES, TILE).transpose(1, 0, 2)

    def one_tile(pair):
        states_tile, ids = pair
        dims = block_dim[ids]
        scales = (BS - 1) * jnp.exp2(-block_level[ids].astype(jnp.float32))
        scaled = scales[:, None] * states_tile[dims]
        lower = jnp.clip(jnp.floor(scaled), 0, BS - 2)
        phi_low = jnp.maximum(0.0, 1.0 - jnp.abs(scaled - lower)).astype(jnp.bfloat16)
        phi_high = jnp.maximum(0.0, 1.0 - jnp.abs(scaled - lower - 1.0)).astype(jnp.bfloat16)
        column = ids.astype(jnp.int32)[:, None] * BS + lower.astype(jnp.int32)
        coef_low = table[:, column].astype(jnp.float32)
        coef_high = table[:, column + 1].astype(jnp.float32)
        terms = phi_low.astype(jnp.float32)[None] * coef_low + phi_high.astype(jnp.float32)[None] * coef_high
        return jnp.sum(terms, axis=1)

    values = lax.map(one_tile, (states_tiles, block_ids))
    log_savings = values.transpose(1, 0, 2).reshape(S * GEN, POINTS)
    savings = jnp.exp(log_savings).astype(jnp.bfloat16).reshape(S, GEN, POINTS)
    capital = jnp.mean(savings.astype(jnp.float32), axis=1)
    interest = 0.33 * tfp[:, None] * capital ** (0.33 - 1.0) + 1.0 - 0.1
    earnings = (1.0 - 0.33) * tfp[:, None] * capital ** 0.33
    transition = trans_weight / jnp.sum(trans_weight, axis=1, keepdims=True)
    onehot = (shock[None, :] == jnp.arange(S, dtype=jnp.int32)[:, None]).astype(jnp.float32)
    weights = jnp.dot(transition.T, onehot, precision=lax.Precision.HIGHEST)
    prices = jnp.stack([jnp.sum(weights * interest, axis=0), jnp.sum(weights * earnings, axis=0)])
    return savings, prices
```

```python
import functools

import jax
import jax.numpy as jnp
from jax import lax
from jax.experimental import pallas as pl
from jax.experimental.pallas import tpu as pltpu
from jax.sharding import PartitionSpec as P

MESH = pl.DeviceIdType.MESH


def gather_kernel(piece, fine, G, F, zs, zr, xs, xr, ys, yr, ss, sr, fs, fr, ls):
    p, g = lax.axis_index("pts"), lax.axis_index("grp")
    c, zl, x, y = p % 2, (p // 2) % 4, (p // 8) % 4, p // 32
    z = g * 4 + zl
    def dev(x, y, z, c):
        return {"pts": ((y * 4 + x) * 4 + z % 4) * 2 + c, "grp": z // 4}
    zd = lambda d: dev(x, y, (z + d + 8) % 8, c)
    xd = lambda d: dev((x + d + 4) % 4, y, z, c)
    yd = lambda d: dev(x, (y + d + 4) % 4, z, c)
    sib = dev(x, y, z, 1 - c)
    zo, xo = (4, 3, -3, 2, -2, 1, -1), (2, 1, -1)
    b = pltpu.get_barrier_semaphore()
    partners = [zd(d) for d in zo] + [xd(d) for d in xo] + [yd(d) for d in xo] + [sib]
    for d in partners:
        pl.semaphore_signal(b, 1, device_id=d, device_id_type=MESH)
    pl.semaphore_wait(b, len(partners))
    pend = []
    def rc(src, dst, s, r, d):
        cp = pltpu.make_async_remote_copy(src, dst, s, r, device_id=d, device_id_type=MESH)
        cp.start()
        pend.append(cp)
        return cp
    own = pltpu.make_async_copy(piece, G.at[c, z, y, x], ls)
    zc = [rc(piece, G.at[c, z, y, x], zs.at[i], zr.at[i], zd(d)) for i, d in enumerate(zo)]
    own.start()
    rc(fine, F, fs, fr, zd(4))
    own.wait()
    for cp in zc: cp.wait_recv()
    a = G.at[c, pl.ds(0, 4), y, x]
    bb = G.at[c, pl.ds(4, 4), y, x]
    s1 = []
    for i, d in enumerate(xo):
        s1.append(rc(a, a, xs.at[i], xr.at[i], xd(d)))
        s1.append(rc(bb, bb, ys.at[i], yr.at[i], yd(d)))
    for cp in s1: cp.wait_recv()
    def A(yy, z0=0, nz=4): return G.at[c, pl.ds(z0, nz), yy]
    def B(xx, z0=4, nz=4): return G.at[c, pl.ds(z0, nz), :, xx]
    def sibs(i, ref): rc(ref, ref, ss.at[i], sr.at[i], sib)
    ym, yp, xm, xp = (y + 3) % 4, (y + 1) % 4, (x + 3) % 4, (x + 1) % 4
    y2, x2 = (y + 2) % 4, (x + 2) % 4
    u = [rc(A(y), A(y), ys.at[3], yr.at[3], yd(1)), rc(B(x), B(x), xs.at[3], xr.at[3], xd(1)),
         rc(A(y), A(y), ys.at[4], yr.at[4], yd(-1)), rc(B(x), B(x), xs.at[4], xr.at[4], xd(-1))]
    sibs(0, A(y)); sibs(1, B(x))
    v = []
    u[0].wait_recv(); v.append(rc(A(ym, 0, 2), A(ym, 0, 2), ys.at[5], yr.at[5], yd(1))); sibs(2, A(ym))
    u[1].wait_recv(); v.append(rc(B(xm, 4, 2), B(xm, 4, 2), xs.at[5], xr.at[5], xd(1))); sibs(3, B(xm))
    u[2].wait_recv(); v.append(rc(A(yp, 2, 2), A(yp, 2, 2), ys.at[6], yr.at[6], yd(-1))); sibs(4, A(yp))
    u[3].wait_recv(); v.append(rc(B(xp, 6, 2), B(xp, 6, 2), xs.at[6], xr.at[6], xd(-1))); sibs(5, B(xp))
    for cp in v: cp.wait_recv()
    sibs(6, A(y2)); sibs(7, B(x2))
    done = set(id(q) for q in zc + s1 + u + v)
    for cp in pend:
        cp.wait_send()
        if id(cp) not in done: cp.wait_recv()

def gather(piece, fine):
    dma = pltpu.SemaphoreType.DMA
    return pl.pallas_call(gather_kernel,
        out_shape=(jax.ShapeDtypeStruct((2,8,4,4,128,128), jnp.bfloat16), jax.ShapeDtypeStruct((30,4,4096), jnp.bfloat16)),
        in_specs=[pl.BlockSpec(memory_space=pl.ANY)]*2, out_specs=[pl.BlockSpec(memory_space=pl.ANY)]*2,
        scratch_shapes=[dma((7,)), dma((7,)), dma((7,)), dma((7,)), dma((7,)), dma((7,)), dma((8,)), dma((8,)), dma, dma, dma],
        compiler_params=pltpu.CompilerParams(collective_id=0, has_side_effects=True))(piece, fine)


TPS = 8

def hat_rows(states, lane0, dim, level, low_ref):
    row = jnp.broadcast_to(states[pl.ds(lane0 * 64 + dim, 1), :], (16, 128))
    scale = jnp.where(level == 0, 127.0, jnp.where(level == 1, 63.5, 31.75))
    scaled = row * scale
    lower = jnp.clip(jnp.floor(scaled), 0.0, 126.0)
    lo = jnp.maximum(0.0, 1.0 - jnp.abs(scaled - lower)).astype(jnp.bfloat16)
    hi = jnp.maximum(0.0, 1.0 - jnp.abs(scaled - lower - 1.0)).astype(jnp.bfloat16)
    at = lower.astype(jnp.bfloat16)
    out = []
    zero = jnp.zeros((16, 128), jnp.bfloat16)
    for q in range(8):
        j = low_ref[pl.ds(16 * q, 16), :]
        t = j - at
        out.append(jnp.where(t == 0, lo, jnp.where(t == 1, hi, zero)))
    return jnp.concatenate(out, axis=0)

def eval_kernel(cid, fid, cdim, clev, fdim, flev, tfp, tw, G, Fo, Fx, states, shock, g_ref, sav, prices, T, J, cap, ST):
    step = pl.program_id(0)
    @pl.when(step == 0)
    def _():
        J[...] = lax.broadcasted_iota(jnp.int32, (128, 128), 0).astype(jnp.float32).astype(jnp.bfloat16)
        own = g_ref[0]
        for k in range(32):
            o = Fo[:, :, pl.ds(128 * k, 128)].reshape(120, 128)
            f = Fx[:, :, pl.ds(128 * k, 128)].reshape(120, 128)
            T[own, k, pl.ds(0, 120), :] = o
            T[1 - own, k, pl.ds(0, 120), :] = f
    for i in range(TPS):
        ST[pl.ds(64 * i, 59), :] = states[:, pl.ds(128 * i, 128)]
    def tile(i, _):
        t = step * TPS + i
        lane0 = pl.multiple_of(i * 128, 128)
        phis, left = [], [[], []]
        for k in range(8):
            b = cid[t * 8 + k]
            phis.append(hat_rows(ST, i, cdim[b], clev[b], J))
            at = ((b % 2) * 8 + (b // 2) % 4) * 16 + (b // 32) * 4 + (b // 8) % 4
            left[0].append(G[at, pl.ds(0, 120), :])
            left[1].append(G[at + 64, pl.ds(0, 120), :])
        for k in range(8):
            b = fid[t * 8 + k]
            phis.append(hat_rows(ST, i, fdim[b], flev[b], J))
            left[0].append(T[0, b, pl.ds(0, 120), :])
            left[1].append(T[1, b, pl.ds(0, 120), :])
        phi = jnp.concatenate(phis, axis=0)
        total = jnp.zeros((8, 128), jnp.float32)
        for h in range(2):
            acc = jnp.dot(jnp.concatenate(left[h], axis=1), phi, preferred_element_type=jnp.float32)
            s = jnp.exp(acc).astype(jnp.bfloat16)
            sav[pl.ds(30 * h, 30), :, pl.ds(lane0, 128)] = s.reshape(30, 4, 128)
            total += jnp.sum(s.astype(jnp.float32).reshape(15, 8, 128), axis=0)
        cap[:, pl.ds(lane0, 128)] = (total[:4] + total[4:])
        return 0
    lax.fori_loop(0, TPS, tile, 0)
    W = TPS * 128
    capital = cap[...] * (1.0 / 60.0)
    sub = lax.broadcasted_iota(jnp.int32, (4, W), 0)
    tf = jnp.where(sub == 0, tfp[0], jnp.where(sub == 1, tfp[1], jnp.where(sub == 2, tfp[2], tfp[3])))
    logc = jnp.log(capital)
    interest = 0.33 * tf * jnp.exp(logc * (0.33 - 1.0)) + 1.0 - 0.1
    earnings = (1.0 - 0.33) * tf * jnp.exp(logc * 0.33)
    sh = jnp.concatenate([shock[pl.ds(step * TPS + i, 1), :] for i in range(TPS)], axis=1)
    w = jnp.zeros((4, W), jnp.float32)
    for k in range(4):
        col = jnp.where(sub == 0, tw[k * 4], jnp.where(sub == 1, tw[k * 4 + 1], jnp.where(sub == 2, tw[k * 4 + 2], tw[k * 4 + 3])))
        den = tw[k * 4] + tw[k * 4 + 1] + tw[k * 4 + 2] + tw[k * 4 + 3]
        w = jnp.where(sh == k, col / den, w)
    prices[0:1, :] = jnp.sum(w * interest, axis=0, keepdims=True)
    prices[1:2, :] = jnp.sum(w * earnings, axis=0, keepdims=True)

def evaluate(cid, fid, cdim, clev, fdim, flev, tfp, tw, G, Fo, Fx, states, shock, g):
    n = states.shape[1]
    steps = n // (TPS * 128)
    smem = pl.BlockSpec(memory_space=pltpu.SMEM)
    vmem = pl.BlockSpec(memory_space=pltpu.VMEM)
    sav, prices = pl.pallas_call(
        eval_kernel,
        grid=(steps,),
        out_shape=(jax.ShapeDtypeStruct((60, 4, n), jnp.bfloat16), jax.ShapeDtypeStruct((2, n), jnp.float32)),
        in_specs=[smem] * 8 + [vmem] * 3 + [pl.BlockSpec((59, TPS * 128), lambda i: (0, i)), vmem, smem],
        out_specs=(pl.BlockSpec((60, 4, TPS * 128), lambda i: (0, 0, i)), pl.BlockSpec((2, TPS * 128), lambda i: (0, i))),
        scratch_shapes=[pltpu.VMEM((2, 32, 128, 128), jnp.bfloat16), pltpu.VMEM((128, 128), jnp.bfloat16), pltpu.VMEM((4, TPS * 128), jnp.float32), pltpu.VMEM((TPS * 64, 128), jnp.float32)],
        compiler_params=pltpu.CompilerParams(vmem_limit_bytes=60 << 20),
        name="evaluate",
    )(cid, fid, cdim, clev, fdim, flev, tfp, tw, G, Fo, Fx, states, shock, g)
    return sav, prices


def body(
    grid_states,
    coarse_active,
    fine_active,
    shock,
    coarse_surplus,
    fine_surplus,
    coarse_dim,
    coarse_level,
    fine_dim,
    fine_level,
    tfp,
    trans_weight,
):
    coarse = coarse_surplus.transpose(1, 0, 2).reshape(120, 128)
    rows = lax.broadcasted_iota(jnp.int32, (8, 128), 0)
    described = jnp.where(rows == 0, coarse_dim[0], coarse_level[0]).astype(jnp.bfloat16)
    piece = jnp.concatenate([coarse, described], axis=0)
    fine = fine_surplus.transpose(1, 0, 2)
    gathered, other = gather(piece, fine)
    told = gathered[:, :4, :, :, 120:122, 0].transpose(2, 3, 1, 0, 4).reshape(128, 2).astype(jnp.int32)
    savings, prices = evaluate(
        coarse_active.reshape(-1),
        fine_active.reshape(-1),
        told[:, 0],
        told[:, 1],
        fine_dim,
        fine_level,
        tfp,
        trans_weight.reshape(-1),
        gathered.reshape(256, 128, 128),
        fine,
        other,
        grid_states,
        shock.reshape(-1, 128),
        lax.axis_index("grp").reshape(1).astype(jnp.int32),
    )
    return (savings.transpose(1, 0, 2), prices)


def solution(mesh):
    in_specs = (
        P(None, ("pts", "grp")),
        P(("pts", "grp"), None),
        P(("pts", "grp"), None),
        P(("pts", "grp")),
        P(None, "grp", "pts"),
        P(None, "grp", "pts"),
        P("pts"),
        P("pts"),
        P("pts"),
        P("pts"),
        P(),
        P(),
    )
    out_specs = (P(None, None, ("pts", "grp")), P(None, ("pts", "grp")))
    return jax.shard_map(body, mesh=mesh, in_specs=in_specs, out_specs=out_specs, check_vma=False)
```

```python
import functools

import jax
import jax.numpy as jnp
from jax import lax
from jax.experimental import pallas as pl
from jax.experimental.pallas import tpu as pltpu
from jax.sharding import PartitionSpec as P

MESH = pl.DeviceIdType.MESH


def gather_kernel(piece, fine, G, F, zs, zr, xs, xr, ys, yr, ss, sr, fs, fr, ls):
    p, g = lax.axis_index("pts"), lax.axis_index("grp")
    c, zl, x, y = p % 2, (p // 2) % 4, (p // 8) % 4, p // 32
    z = g * 4 + zl
    def dev(x, y, z, c):
        return {"pts": ((y * 4 + x) * 4 + z % 4) * 2 + c, "grp": z // 4}
    zd = lambda d: dev(x, y, (z + d + 8) % 8, c)
    xd = lambda d: dev((x + d + 4) % 4, y, z, c)
    yd = lambda d: dev(x, (y + d + 4) % 4, z, c)
    sib = dev(x, y, z, 1 - c)
    zo, xo = (4, 3, -3, 2, -2, 1, -1), (2, 1, -1)
    b = pltpu.get_barrier_semaphore()
    partners = [zd(d) for d in zo] + [xd(d) for d in xo] + [yd(d) for d in xo] + [sib]
    for d in partners:
        pl.semaphore_signal(b, 1, device_id=d, device_id_type=MESH)
    pl.semaphore_wait(b, len(partners))
    pend = []
    def rc(src, dst, s, r, d):
        cp = pltpu.make_async_remote_copy(src, dst, s, r, device_id=d, device_id_type=MESH)
        cp.start()
        pend.append(cp)
        return cp
    own = pltpu.make_async_copy(piece, G.at[g, y, x, zl, c], ls)
    zc = [rc(piece, G.at[g, y, x, zl, c], zs.at[i], zr.at[i], zd(d)) for i, d in enumerate(zo)]
    own.start()
    rc(fine, F, fs, fr, zd(4))
    own.wait()
    for cp in zc: cp.wait_recv()
    a = G.at[0, y, x, :, c]
    bb = G.at[1, y, x, :, c]
    s1 = []
    for i, d in enumerate(xo):
        s1.append(rc(a, a, xs.at[i], xr.at[i], xd(d)))
        s1.append(rc(bb, bb, ys.at[i], yr.at[i], yd(d)))
    for cp in s1: cp.wait_recv()
    def A(yy, z0=0, nz=4): return G.at[0, yy, :, pl.ds(z0, nz), c]
    def B(xx, z0=0, nz=4): return G.at[1, :, xx, pl.ds(z0, nz), c]
    def sibs(i, ref): rc(ref, ref, ss.at[i], sr.at[i], sib)
    ym, yp, xm, xp = (y + 3) % 4, (y + 1) % 4, (x + 3) % 4, (x + 1) % 4
    y2, x2 = (y + 2) % 4, (x + 2) % 4
    u = [rc(A(y), A(y), ys.at[3], yr.at[3], yd(1)), rc(B(x), B(x), xs.at[3], xr.at[3], xd(1)),
         rc(A(y), A(y), ys.at[4], yr.at[4], yd(-1)), rc(B(x), B(x), xs.at[4], xr.at[4], xd(-1))]
    sibs(0, A(y)); sibs(1, B(x))
    v = []
    u[0].wait_recv(); v.append(rc(A(ym, 0, 2), A(ym, 0, 2), ys.at[5], yr.at[5], yd(1))); sibs(2, A(ym))
    u[1].wait_recv(); v.append(rc(B(xm, 0, 2), B(xm, 0, 2), xs.at[5], xr.at[5], xd(1))); sibs(3, B(xm))
    u[2].wait_recv(); v.append(rc(A(yp, 2, 2), A(yp, 2, 2), ys.at[6], yr.at[6], yd(-1))); sibs(4, A(yp))
    u[3].wait_recv(); v.append(rc(B(xp, 2, 2), B(xp, 2, 2), xs.at[6], xr.at[6], xd(-1))); sibs(5, B(xp))
    for cp in v: cp.wait_recv()
    sibs(6, A(y2)); sibs(7, B(x2))
    done = set(id(q) for q in zc + s1 + u + v)
    for cp in pend:
        cp.wait_send()
        if id(cp) not in done: cp.wait_recv()

def gather(piece, fine):
    dma = pltpu.SemaphoreType.DMA
    return pl.pallas_call(gather_kernel,
        out_shape=(jax.ShapeDtypeStruct((2, 4, 4, 4, 2, 128, 128), jnp.bfloat16), jax.ShapeDtypeStruct((30,4,4096), jnp.bfloat16)),
        in_specs=[pl.BlockSpec(memory_space=pl.ANY)]*2, out_specs=[pl.BlockSpec(memory_space=pl.ANY)]*2,
        scratch_shapes=[dma((7,)), dma((7,)), dma((7,)), dma((7,)), dma((7,)), dma((7,)), dma((8,)), dma((8,)), dma, dma, dma],
        compiler_params=pltpu.CompilerParams(collective_id=0, has_side_effects=True))(piece, fine)


def ACC(m):
    return pltpu.ACC(m)((128, 256), jnp.float32)

TPS = 8

def hat_rows(states, lane0, dim, level, low_ref):
    row = jnp.broadcast_to(states[pl.ds(lane0 * 64 + dim, 1), :], (8, 128))
    scale = jnp.where(level == 0, 127.0, jnp.where(level == 1, 63.5, 31.75))
    scaled = row * scale
    lower = jnp.minimum(jnp.floor(scaled), 126.0)
    part = scaled - lower
    twice = lambda v: jnp.concatenate([v, v], axis=0).astype(jnp.bfloat16)
    lo = twice(1.0 - part)
    hi = twice(1.0 - jnp.abs(part - 1.0))
    at, nx = twice(lower), twice(lower + 1.0)
    out = []
    zero = jnp.zeros((16, 128), jnp.bfloat16)
    for q in range(8):
        j = low_ref[pl.ds(16 * q, 16), :]
        out.append(jnp.where(j == at, lo, jnp.where(j == nx, hi, zero)))
    return jnp.concatenate(out, axis=0)

def eval_kernel(cid, fid, fdim, flev, tfp, tw, G, Fo, Fx, states, shock, g_ref, sav, prices, T, J, cap, ST, told_v, told, told_sem):
    step = pl.program_id(0)
    @pl.when(step == 0)
    def _():
        J[...] = lax.broadcasted_iota(jnp.int32, (128, 128), 0).astype(jnp.float32).astype(jnp.bfloat16)
        lane = lax.broadcasted_iota(jnp.int32, (8, 128), 1)
        said = jnp.zeros((8, 128), jnp.float32)
        for b in range(128):
            said = jnp.where(lane == b, G[b, pl.ds(120, 8), :].astype(jnp.float32), said)
        told_v[...] = said.astype(jnp.int32)
        telling = pltpu.make_async_copy(told_v, told, told_sem)
        telling.start()
        own = g_ref[0]
        for k in range(32):
            o = Fo[:, :, pl.ds(128 * k, 128)].reshape(120, 128)
            f = Fx[:, :, pl.ds(128 * k, 128)].reshape(120, 128)
            T[own, k, pl.ds(0, 120), :] = o
            T[1 - own, k, pl.ds(0, 120), :] = f
        telling.wait()
    for i in range(TPS):
        ST[pl.ds(64 * i, 59), :] = states[:, pl.ds(128 * i, 128)]
    def tile(accs, ii, _):
        i = ii * 2
        t = step * TPS + i
        lane0 = i * 128
        def pair(t, i, q):
            phis, left = [], [[], []]
            for k in (2 * q, 2 * q + 1):
                if k < 8:
                    b = cid[k, t]
                    phis.append(hat_rows(ST, i, told[0, b], told[1, b], J))
                    left[0].append(G[b])
                    left[1].append(G[b + 128])
                else:
                    b = fid[k - 8, t]
                    phis.append(hat_rows(ST, i, fdim[b], flev[b], J))
                    left[0].append(T[0, b])
                    left[1].append(T[1, b])
            return jnp.concatenate(phis, axis=0), [jnp.concatenate(l, axis=1) for l in left]
        for q in range(8):
            for m in range(2):
                phi, left = pair(t + m, i + m, q)
                pltpu.matmul_push_rhs(jnp.concatenate([phi, phi], axis=1), q % 2, m)
                for h in range(2):
                    pltpu.matmul_acc_lhs(accs[m][h], left[h], load_staged_rhs=q % 2 if h == 0 else None)
        for m in range(2):
            lane = lane0 + m * 128
            total = jnp.zeros((8, 128), jnp.float32)
            for h in range(2):
                a = pltpu.matmul_pop(accs[m][h])[:120, :128]
                s = jnp.exp(a).astype(jnp.bfloat16)
                sav[pl.ds(30 * h, 30), :, pl.ds(lane, 128)] = s.reshape(30, 4, 128)
                total += jnp.sum(s.astype(jnp.float32).reshape(15, 8, 128), axis=0)
            cap[:, pl.ds(lane, 128)] = (total[:4] + total[4:])
        return 0
    def scoped(*a):
        for ii in range(TPS // 2):
            o = 4 * (ii % 2)
            tile([[a[o], a[o + 1]], [a[o + 2], a[o + 3]]], ii, 0)
    pl.run_scoped(scoped, *([ACC(0), ACC(0), ACC(1), ACC(1)] * 2))
    W = TPS * 128
    capital = cap[...] * (1.0 / 60.0)
    sub = lax.broadcasted_iota(jnp.int32, (4, W), 0)
    tf = jnp.where(sub == 0, tfp[0], jnp.where(sub == 1, tfp[1], jnp.where(sub == 2, tfp[2], tfp[3])))
    logc = jnp.log(capital)
    interest = 0.33 * tf * jnp.exp(logc * (0.33 - 1.0)) + 1.0 - 0.1
    earnings = (1.0 - 0.33) * tf * jnp.exp(logc * 0.33)
    sh = jnp.concatenate([shock[pl.ds(step * TPS + i, 1), :] for i in range(TPS)], axis=1)
    w = jnp.zeros((4, W), jnp.float32)
    for k in range(4):
        col = jnp.where(sub == 0, tw[k, 0], jnp.where(sub == 1, tw[k, 1], jnp.where(sub == 2, tw[k, 2], tw[k, 3])))
        den = tw[k, 0] + tw[k, 1] + tw[k, 2] + tw[k, 3]
        w = jnp.where(sh == k, col / den, w)
    prices[0:1, :] = jnp.sum(w * interest, axis=0, keepdims=True)
    prices[1:2, :] = jnp.sum(w * earnings, axis=0, keepdims=True)

def evaluate(cid, fid, fdim, flev, tfp, tw, G, Fo, Fx, states, shock, g):
    n = states.shape[1]
    steps = n // (TPS * 128)
    smem = pl.BlockSpec(memory_space=pltpu.SMEM)
    vmem = pl.BlockSpec(memory_space=pltpu.VMEM)
    sav, prices = pl.pallas_call(
        eval_kernel,
        grid=(steps,),
        out_shape=(jax.ShapeDtypeStruct((60, 4, n), jnp.bfloat16), jax.ShapeDtypeStruct((2, n), jnp.float32)),
        in_specs=[smem] * 6 + [vmem] * 3 + [pl.BlockSpec((59, TPS * 128), lambda i: (0, i)), vmem, smem],
        out_specs=(pl.BlockSpec((60, 4, TPS * 128), lambda i: (0, 0, i)), pl.BlockSpec((2, TPS * 128), lambda i: (0, i))),
        scratch_shapes=[pltpu.VMEM((2, 32, 128, 128), jnp.bfloat16), pltpu.VMEM((128, 128), jnp.bfloat16), pltpu.VMEM((4, TPS * 128), jnp.float32), pltpu.VMEM((TPS * 64, 128), jnp.float32), pltpu.VMEM((8, 128), jnp.int32), pltpu.SMEM((8, 128), jnp.int32), pltpu.SemaphoreType.DMA],
        compiler_params=pltpu.CompilerParams(vmem_limit_bytes=60 << 20),
        name="evaluate",
    )(cid, fid, fdim, flev, tfp, tw, G, Fo, Fx, states, shock, g)
    return sav, prices


def body(
    grid_states,
    coarse_active,
    fine_active,
    shock,
    coarse_surplus,
    fine_surplus,
    coarse_dim,
    coarse_level,
    fine_dim,
    fine_level,
    tfp,
    trans_weight,
):
    coarse = coarse_surplus.transpose(1, 0, 2).reshape(120, 128)
    rows = lax.broadcasted_iota(jnp.int32, (8, 128), 0)
    described = jnp.where(rows == 0, coarse_dim[0], coarse_level[0]).astype(jnp.bfloat16)
    piece = jnp.concatenate([coarse, described], axis=0)
    fine = fine_surplus.transpose(1, 0, 2)
    gathered, other = gather(piece, fine)
    savings, prices = evaluate(
        coarse_active.T,
        fine_active.T,
        fine_dim,
        fine_level,
        tfp,
        trans_weight,
        gathered.reshape(256, 128, 128),
        fine,
        other,
        grid_states,
        shock.reshape(-1, 128),
        lax.axis_index("grp").reshape(1).astype(jnp.int32),
    )
    return (savings.transpose(1, 0, 2), prices)


def solution(mesh):
    in_specs = (
        P(None, ("pts", "grp")),
        P(("pts", "grp"), None),
        P(("pts", "grp"), None),
        P(("pts", "grp")),
        P(None, "grp", "pts"),
        P(None, "grp", "pts"),
        P("pts"),
        P("pts"),
        P("pts"),
        P("pts"),
        P(),
        P(),
    )
    out_specs = (P(None, None, ("pts", "grp")), P(None, ("pts", "grp")))
    step = jax.shard_map(body, mesh=mesh, in_specs=in_specs, out_specs=out_specs, check_vma=False)

    def run(*args):
        with jax.sharding.use_abstract_mesh(mesh.abstract_mesh):
            return step(*args)

    return run
```

```python
import functools

import jax
import jax.numpy as jnp
from jax import lax
from jax.experimental import pallas as pl
from jax.experimental.pallas import tpu as pltpu
from jax.sharding import PartitionSpec as P

MESH = pl.DeviceIdType.MESH


def stay(v):
    return pltpu.with_memory_space_constraint(v, pltpu.HBM)


def gather_kernel(piece, fine, G, F, zs, zr, xs, xr, ys, yr, ss, sr, fs, fr, ls):
    p, g = lax.axis_index("pts"), lax.axis_index("grp")
    c, zl, x, y = p % 2, (p // 2) % 4, (p // 8) % 4, p // 32
    z = g * 4 + zl
    def dev(x, y, z, c):
        return {"pts": ((y * 4 + x) * 4 + z % 4) * 2 + c, "grp": z // 4}
    zd = lambda d: dev(x, y, (z + d + 8) % 8, c)
    xd = lambda d: dev((x + d + 4) % 4, y, z, c)
    yd = lambda d: dev(x, (y + d + 4) % 4, z, c)
    sib = dev(x, y, z, 1 - c)
    zo, xo = (4, 3, -3, 2, -2, 1, -1), (2, 1, -1)
    b = pltpu.get_barrier_semaphore()
    partners = [zd(d) for d in zo] + [xd(d) for d in xo] + [yd(d) for d in xo] + [sib]
    for d in partners:
        pl.semaphore_signal(b, 1, device_id=d, device_id_type=MESH)
    pl.semaphore_wait(b, len(partners))
    pend = []
    def rc(src, dst, s, r, d):
        cp = pltpu.make_async_remote_copy(src, dst, s, r, device_id=d, device_id_type=MESH)
        cp.start()
        pend.append(cp)
        return cp
    own = pltpu.make_async_copy(piece, G.at[g, y, x, zl, c], ls)
    zc = [rc(piece, G.at[g, y, x, zl, c], zs.at[i], zr.at[i], zd(d)) for i, d in enumerate(zo)]
    own.start()
    rc(fine, F, fs, fr, zd(4))
    own.wait()
    for cp in zc: cp.wait_recv()
    a = G.at[0, y, x, :, c]
    bb = G.at[1, y, x, :, c]
    s1 = []
    for i, d in enumerate(xo):
        s1.append(rc(a, a, xs.at[i], xr.at[i], xd(d)))
        s1.append(rc(bb, bb, ys.at[i], yr.at[i], yd(d)))
    for cp in s1: cp.wait_recv()
    def A(yy, z0=0, nz=4): return G.at[0, yy, :, pl.ds(z0, nz), c]
    def B(xx, z0=0, nz=4): return G.at[1, :, xx, pl.ds(z0, nz), c]
    def sibs(i, ref): rc(ref, ref, ss.at[i], sr.at[i], sib)
    ym, yp, xm, xp = (y + 3) % 4, (y + 1) % 4, (x + 3) % 4, (x + 1) % 4
    y2, x2 = (y + 2) % 4, (x + 2) % 4
    u = [rc(A(y), A(y), ys.at[3], yr.at[3], yd(1)), rc(B(x), B(x), xs.at[3], xr.at[3], xd(1)),
         rc(A(y), A(y), ys.at[4], yr.at[4], yd(-1)), rc(B(x), B(x), xs.at[4], xr.at[4], xd(-1))]
    sibs(0, A(y)); sibs(1, B(x))
    v = []
    u[0].wait_recv(); v.append(rc(A(ym, 0, 2), A(ym, 0, 2), ys.at[5], yr.at[5], yd(1))); sibs(2, A(ym))
    u[1].wait_recv(); v.append(rc(B(xm, 0, 2), B(xm, 0, 2), xs.at[5], xr.at[5], xd(1))); sibs(3, B(xm))
    u[2].wait_recv(); v.append(rc(A(yp, 2, 2), A(yp, 2, 2), ys.at[6], yr.at[6], yd(-1))); sibs(4, A(yp))
    u[3].wait_recv(); v.append(rc(B(xp, 2, 2), B(xp, 2, 2), xs.at[6], xr.at[6], xd(-1))); sibs(5, B(xp))
    for cp in v: cp.wait_recv()
    sibs(6, A(y2)); sibs(7, B(x2))
    done = set(id(q) for q in zc + s1 + u + v)
    for cp in pend:
        cp.wait_send()
        if id(cp) not in done: cp.wait_recv()

def gather(piece, fine):
    dma = pltpu.SemaphoreType.DMA
    return pl.pallas_call(gather_kernel,
        out_shape=(jax.ShapeDtypeStruct((2, 4, 4, 4, 2, 128, 128), jnp.bfloat16), jax.ShapeDtypeStruct((30,4,4096), jnp.bfloat16)),
        in_specs=[pl.BlockSpec(memory_space=pl.ANY)]*2, out_specs=[pl.BlockSpec(memory_space=pltpu.VMEM)]*2,
        scratch_shapes=[dma((7,)), dma((7,)), dma((7,)), dma((7,)), dma((7,)), dma((7,)), dma((8,)), dma((8,)), dma, dma, dma],
        compiler_params=pltpu.CompilerParams(collective_id=0, has_side_effects=True, vmem_limit_bytes=16 << 20))(piece, stay(fine))


def ACC(m):
    return pltpu.ACC(m)((240, 256), jnp.float32)

TPS = 16

def hat_rows(states, lane0, dim, level, low_ref):
    row = jnp.broadcast_to(states[pl.ds(lane0 * 64 + dim, 1), :], (8, 128))
    scale = jnp.where(level == 0, 127.0, jnp.where(level == 1, 63.5, 31.75))
    scaled = row * scale
    lower = jnp.minimum(jnp.floor(scaled), 126.0)
    part = scaled - lower
    twice = lambda v: jnp.concatenate([v, v], axis=0).astype(jnp.bfloat16)
    lo = twice(1.0 - part)
    hi = twice(1.0 - jnp.abs(part - 1.0))
    at, nx = twice(lower), twice(lower + 1.0)
    out = []
    zero = jnp.zeros((16, 128), jnp.bfloat16)
    for q in range(8):
        j = low_ref[pl.ds(16 * q, 16), :]
        out.append(jnp.where(j == at, lo, jnp.where(j == nx, hi, zero)))
    return jnp.concatenate(out, axis=0)

def eval_kernel(cid, fid, fdim, flev, tfp, tw, G, Fo, Fx, states, shock, g_ref, sav, prices, T, J, cap, ST, told_v, told, told_sem):
    step = pl.program_id(0)
    @pl.when(step == 0)
    def _():
        J[...] = lax.broadcasted_iota(jnp.int32, (128, 128), 0).astype(jnp.float32).astype(jnp.bfloat16)
        lane = lax.broadcasted_iota(jnp.int32, (8, 128), 1)
        said = jnp.zeros((8, 128), jnp.float32)
        for b in range(128):
            said = jnp.where(lane == b, G[b, pl.ds(120, 8), :].astype(jnp.float32), said)
        told_v[...] = said.astype(jnp.int32)
        telling = pltpu.make_async_copy(told_v, told, told_sem)
        telling.start()
        own = g_ref[0]
        for k in range(32):
            o = Fo[:, :, pl.ds(128 * k, 128)].reshape(120, 128)
            f = Fx[:, :, pl.ds(128 * k, 128)].reshape(120, 128)
            T[0, k, pl.ds(0, 120), :] = jnp.where(own == 0, o, f)
            T[1, k, pl.ds(8, 120), :] = jnp.where(own == 0, f, o)
        telling.wait()
    for i in range(TPS):
        ST[pl.ds(64 * i, 59), :] = states[:, pl.ds(128 * i, 128)]
    def tile(accs, ii, _):
        i = ii * 2
        t = step * TPS + i
        lane0 = i * 128
        upper = lax.broadcasted_iota(jnp.int32, (16, 128), 0) < 8
        def rows_of(first, second):
            mixed = jnp.where(upper, first[112:], second[:16])
            return jnp.concatenate([first[:112], mixed, second[16:]], axis=0)
        def pair(t, i, q):
            phis, left = [], []
            for k in (2 * q, 2 * q + 1):
                if k < 8:
                    b = cid[k, t]
                    phis.append(hat_rows(ST, i, told[0, b], told[1, b], J))
                    left.append(rows_of(G[b], G[b + 128]))
                else:
                    b = fid[k - 8, t]
                    phis.append(hat_rows(ST, i, fdim[b], flev[b], J))
                    left.append(rows_of(T[0, b], T[1, b]))
            return jnp.concatenate(phis, axis=0), jnp.concatenate(left, axis=1)
        for q in range(8):
            for m in range(2):
                phi, left = pair(t + m, i + m, q)
                pltpu.matmul_push_rhs(jnp.concatenate([phi, phi], axis=1), q % 2, m)
                pltpu.matmul_acc_lhs(accs[m], left, load_staged_rhs=q % 2)
        for m in range(2):
            lane = lane0 + m * 128
            s = jnp.exp(pltpu.matmul_pop(accs[m])[:, :128]).astype(jnp.bfloat16)
            sav[:, :, pl.ds(lane, 128)] = s.reshape(60, 4, 128)
            total = jnp.sum(s.astype(jnp.float32).reshape(30, 8, 128), axis=0)
            cap[:, pl.ds(lane, 128)] = total[:4] + total[4:]
        return 0
    def scoped(*a):
        for ii in range(TPS // 2):
            o = 2 * (ii % 2)
            tile([a[o], a[o + 1]], ii, 0)
    pl.run_scoped(scoped, *([ACC(0), ACC(1)] * 2))
    W = TPS * 128
    capital = cap[...] * (1.0 / 60.0)
    sub = lax.broadcasted_iota(jnp.int32, (4, W), 0)
    tf = jnp.where(sub == 0, tfp[0], jnp.where(sub == 1, tfp[1], jnp.where(sub == 2, tfp[2], tfp[3])))
    logc = jnp.log(capital)
    interest = 0.33 * tf * jnp.exp(logc * (0.33 - 1.0)) + 1.0 - 0.1
    earnings = (1.0 - 0.33) * tf * jnp.exp(logc * 0.33)
    sh = jnp.concatenate([shock[pl.ds(step * TPS + i, 1), :] for i in range(TPS)], axis=1)
    w = jnp.zeros((4, W), jnp.float32)
    for k in range(4):
        col = jnp.where(sub == 0, tw[k, 0], jnp.where(sub == 1, tw[k, 1], jnp.where(sub == 2, tw[k, 2], tw[k, 3])))
        den = tw[k, 0] + tw[k, 1] + tw[k, 2] + tw[k, 3]
        w = jnp.where(sh == k, col / den, w)
    prices[0:1, :] = jnp.sum(w * interest, axis=0, keepdims=True)
    prices[1:2, :] = jnp.sum(w * earnings, axis=0, keepdims=True)

def evaluate(cid, fid, fdim, flev, tfp, tw, G, Fo, Fx, states, shock, g):
    n = states.shape[1]
    steps = n // (TPS * 128)
    smem = pl.BlockSpec(memory_space=pltpu.SMEM)
    vmem = pl.BlockSpec(memory_space=pltpu.VMEM)
    sav, prices = pl.pallas_call(
        eval_kernel,
        grid=(steps,),
        out_shape=(jax.ShapeDtypeStruct((60, 4, n), jnp.bfloat16), jax.ShapeDtypeStruct((2, n), jnp.float32)),
        in_specs=[smem] * 6 + [vmem] * 3 + [pl.BlockSpec((59, TPS * 128), lambda i: (0, i)), vmem, smem],
        out_specs=(pl.BlockSpec((60, 4, TPS * 128), lambda i: (0, 0, i)), pl.BlockSpec((2, TPS * 128), lambda i: (0, i))),
        scratch_shapes=[pltpu.VMEM((2, 32, 128, 128), jnp.bfloat16), pltpu.VMEM((128, 128), jnp.bfloat16), pltpu.VMEM((4, TPS * 128), jnp.float32), pltpu.VMEM((TPS * 64, 128), jnp.float32), pltpu.VMEM((8, 128), jnp.int32), pltpu.SMEM((8, 128), jnp.int32), pltpu.SemaphoreType.DMA],
        compiler_params=pltpu.CompilerParams(vmem_limit_bytes=40 << 20),
        name="evaluate",
    )(*(stay(v) for v in (cid, fid, fdim, flev, tfp, tw)), G, stay(Fo), Fx, stay(states), stay(shock), g)
    return sav, prices


def body(
    grid_states,
    coarse_active,
    fine_active,
    shock,
    coarse_surplus,
    fine_surplus,
    coarse_dim,
    coarse_level,
    fine_dim,
    fine_level,
    tfp,
    trans_weight,
):
    coarse = coarse_surplus.transpose(1, 0, 2).reshape(120, 128)
    rows = lax.broadcasted_iota(jnp.int32, (8, 128), 0)
    described = jnp.where(rows == 0, coarse_dim[0], coarse_level[0]).astype(jnp.bfloat16)
    piece = jnp.where(
        lax.axis_index("grp") == 0,
        jnp.concatenate([coarse, described], axis=0),
        jnp.concatenate([described, coarse], axis=0),
    )
    fine = fine_surplus.transpose(1, 0, 2)
    gathered, other = gather(piece, fine)
    savings, prices = evaluate(
        coarse_active.T,
        fine_active.T,
        fine_dim,
        fine_level,
        tfp,
        trans_weight,
        gathered.reshape(256, 128, 128),
        fine,
        other,
        grid_states,
        shock.reshape(-1, 128),
        lax.axis_index("grp").reshape(1).astype(jnp.int32),
    )
    return (savings.transpose(1, 0, 2), prices)


def solution(mesh):
    in_specs = (
        P(None, ("pts", "grp")),
        P(("pts", "grp"), None),
        P(("pts", "grp"), None),
        P(("pts", "grp")),
        P(None, "grp", "pts"),
        P(None, "grp", "pts"),
        P("pts"),
        P("pts"),
        P("pts"),
        P("pts"),
        P(),
        P(),
    )
    out_specs = (P(None, None, ("pts", "grp")), P(None, ("pts", "grp")))
    step = jax.shard_map(body, mesh=mesh, in_specs=in_specs, out_specs=out_specs, check_vma=False)

    def run(*args):
        with jax.sharding.use_abstract_mesh(mesh.abstract_mesh):
            return step(*args)

    return run
```

```python
import functools

import jax
import jax.numpy as jnp
from jax import lax
from jax.experimental import pallas as pl
from jax.experimental.pallas import tpu as pltpu
from jax.sharding import PartitionSpec as P

MESH = pl.DeviceIdType.MESH


def own_sums(fid, fdim, flev, fine, states, T, ST, part, quarter):
    def repack(k, _):
        T[k] = fine[:, :, pl.ds(pl.multiple_of(k * 128, 128), 128)].reshape(120, 128)
        return 0
    if quarter == 0:
        lax.fori_loop(0, fine.shape[2] // 128, repack, 0)
    J = basis()
    def tile(t, _):
        ST[pl.ds(0, 59), :] = states[:, pl.ds(pl.multiple_of(t * 128, 128), 128)]
        phis, left = [], []
        for k in range(8):
            b = fid[k, t]
            phis.append(hat_rows(ST, 0, fdim[b], flev[b], J))
            left.append(T[b])
        part[t] = jnp.dot(jnp.concatenate(left, axis=1), jnp.concatenate(phis, axis=0), preferred_element_type=jnp.float32)
        return 0
    size = part.shape[0] // 4
    lax.fori_loop(quarter * size, (quarter + 1) * size, tile, 0)


def basis():
    rows = lax.broadcasted_iota(jnp.int32, (16, 128), 0)
    return [(rows + 16 * q).astype(jnp.float32).astype(jnp.bfloat16) for q in range(8)]


def stay(v):
    return pltpu.with_memory_space_constraint(v, pltpu.HBM)


def gather_kernel(fid, fdim, flev, piece, fine, states, G, F, part, zs, zr, xs, xr, ys, yr, ss, sr, fs, fr, ls, fine_v, states_v, T, ST, cs):
    p, g = lax.axis_index("pts"), lax.axis_index("grp")
    c, zl, x, y = p % 2, (p // 2) % 4, (p // 8) % 4, p // 32
    z = g * 4 + zl
    def dev(x, y, z, c):
        return {"pts": ((y * 4 + x) * 4 + z % 4) * 2 + c, "grp": z // 4}
    zd = lambda d: dev(x, y, (z + d + 8) % 8, c)
    xd = lambda d: dev((x + d + 4) % 4, y, z, c)
    yd = lambda d: dev(x, (y + d + 4) % 4, z, c)
    sib = dev(x, y, z, 1 - c)
    zo, xo = (4, 3, -3, 2, -2, 1, -1), (2, 1, -1)
    b = pltpu.get_barrier_semaphore()
    partners = [zd(d) for d in zo] + [xd(d) for d in xo] + [yd(d) for d in xo] + [sib]
    for d in partners:
        pl.semaphore_signal(b, 1, device_id=d, device_id_type=MESH)
    pl.semaphore_wait(b, len(partners))
    pend = []
    def rc(src, dst, s, r, d):
        cp = pltpu.make_async_remote_copy(src, dst, s, r, device_id=d, device_id_type=MESH)
        cp.start()
        pend.append(cp)
        return cp
    own = pltpu.make_async_copy(piece, G.at[g, y, x, zl, c], ls)
    zc = [rc(piece, G.at[g, y, x, zl, c], zs.at[i], zr.at[i], zd(d)) for i, d in enumerate(zo)]
    own.start()
    rc(fine, F, fs, fr, zd(4))
    loads = [pltpu.make_async_copy(fine, fine_v, cs.at[0]), pltpu.make_async_copy(states, states_v, cs.at[1])]
    for cp in loads: cp.start()
    for cp in loads: cp.wait()
    work = functools.partial(own_sums, fid, fdim, flev, fine_v, states_v, T, ST, part)
    work(0)
    own.wait()
    for cp in zc: cp.wait_recv()
    a = G.at[0, y, x, :, c]
    bb = G.at[1, y, x, :, c]
    s1 = []
    for i, d in enumerate(xo):
        s1.append(rc(a, a, xs.at[i], xr.at[i], xd(d)))
        s1.append(rc(bb, bb, ys.at[i], yr.at[i], yd(d)))
    work(1)
    for cp in s1: cp.wait_recv()
    def A(yy, z0=0, nz=4): return G.at[0, yy, :, pl.ds(z0, nz), c]
    def B(xx, z0=0, nz=4): return G.at[1, :, xx, pl.ds(z0, nz), c]
    def sibs(i, ref): rc(ref, ref, ss.at[i], sr.at[i], sib)
    ym, yp, xm, xp = (y + 3) % 4, (y + 1) % 4, (x + 3) % 4, (x + 1) % 4
    y2, x2 = (y + 2) % 4, (x + 2) % 4
    u = [rc(A(y), A(y), ys.at[3], yr.at[3], yd(1)), rc(B(x), B(x), xs.at[3], xr.at[3], xd(1)),
         rc(A(y), A(y), ys.at[4], yr.at[4], yd(-1)), rc(B(x), B(x), xs.at[4], xr.at[4], xd(-1))]
    sibs(0, A(y)); sibs(1, B(x))
    work(2)
    v = []
    u[0].wait_recv(); v.append(rc(A(ym, 0, 2), A(ym, 0, 2), ys.at[5], yr.at[5], yd(1))); sibs(2, A(ym))
    u[1].wait_recv(); v.append(rc(B(xm, 0, 2), B(xm, 0, 2), xs.at[5], xr.at[5], xd(1))); sibs(3, B(xm))
    u[2].wait_recv(); v.append(rc(A(yp, 2, 2), A(yp, 2, 2), ys.at[6], yr.at[6], yd(-1))); sibs(4, A(yp))
    u[3].wait_recv(); v.append(rc(B(xp, 2, 2), B(xp, 2, 2), xs.at[6], xr.at[6], xd(-1))); sibs(5, B(xp))
    work(3)
    for cp in v: cp.wait_recv()
    sibs(6, A(y2)); sibs(7, B(x2))
    done = set(id(q) for q in zc + s1 + u + v)
    for cp in pend:
        cp.wait_send()
        if id(cp) not in done: cp.wait_recv()

def gather(piece, fine, fid, fdim, flev, states):
    dma = pltpu.SemaphoreType.DMA
    tiles = states.shape[1] // 128
    return pl.pallas_call(
        gather_kernel,
        out_shape=(
            jax.ShapeDtypeStruct((2, 4, 4, 4, 2, 128, 128), jnp.bfloat16),
            jax.ShapeDtypeStruct(fine.shape, jnp.bfloat16),
            jax.ShapeDtypeStruct((tiles, 120, 128), jnp.float32),
        ),
        in_specs=[pl.BlockSpec(memory_space=pltpu.SMEM)] * 3 + [pl.BlockSpec(memory_space=pl.ANY)] * 3,
        out_specs=[pl.BlockSpec(memory_space=pltpu.VMEM)] * 3,
        scratch_shapes=[dma((7,)), dma((7,)), dma((7,)), dma((7,)), dma((7,)), dma((7,)), dma((8,)), dma((8,)), dma, dma, dma]
        + [pltpu.VMEM(fine.shape, jnp.bfloat16), pltpu.VMEM(states.shape, jnp.float32), pltpu.VMEM((32, 120, 128), jnp.bfloat16), pltpu.VMEM((64, 128), jnp.float32), dma((2,))],
        compiler_params=pltpu.CompilerParams(collective_id=0, has_side_effects=True, vmem_limit_bytes=24 << 20),
        name="gather",
    )(stay(fid), stay(fdim), stay(flev), piece, stay(fine), stay(states))


def ACC(m, rows):
    return pltpu.ACC(m)((rows, 256), jnp.float32)

TPS = 16

def hat_rows(states, lane0, dim, level, low_ref):
    row = jnp.broadcast_to(states[pl.ds(lane0 * 64 + dim, 1), :], (8, 128))
    scale = jnp.where(level == 0, 127.0, jnp.where(level == 1, 63.5, 31.75))
    scaled = row * scale
    lower = jnp.minimum(jnp.floor(scaled), 126.0)
    part = scaled - lower
    twice = lambda v: jnp.concatenate([v, v], axis=0).astype(jnp.bfloat16)
    lo = twice(1.0 - part)
    hi = twice(1.0 - jnp.abs(part - 1.0))
    at, nx = twice(lower), twice(lower + 1.0)
    out = []
    zero = jnp.zeros((16, 128), jnp.bfloat16)
    for q in range(8):
        j = low_ref[q]
        out.append(jnp.where(j == at, lo, jnp.where(j == nx, hi, zero)))
    return jnp.concatenate(out, axis=0)

def eval_kernel(cid, fid, fdim, flev, tfp, tw, G, Fx, part, states, shock, g_ref, sav, prices, T, cap, ST, FS, told_v, told, told_sem):
    step = pl.program_id(0)
    @pl.when(step == 0)
    def _():
        lane = lax.broadcasted_iota(jnp.int32, (8, 128), 1)
        said = jnp.zeros((8, 128), jnp.float32)
        for b in range(128):
            said = jnp.where(lane == b, G[b, pl.ds(120, 8), :].astype(jnp.float32), said)
        told_v[...] = said.astype(jnp.int32)
        telling = pltpu.make_async_copy(told_v, told, told_sem)
        telling.start()
        for k in range(32):
            T[k, pl.ds(0, 120), :] = Fx[:, :, pl.ds(128 * k, 128)].reshape(120, 128)
        telling.wait()
    for i in range(TPS):
        ST[pl.ds(64 * i, 59), :] = states[:, pl.ds(128 * i, 128)]
    J = basis()
    mine = g_ref[0] == 0

    def tile(accs, fines, ii, _):
        i = ii * 2
        t = step * TPS + i
        lane0 = i * 128
        upper = lax.broadcasted_iota(jnp.int32, (16, 128), 0) < 8
        def rows_of(first, second):
            mixed = jnp.where(upper, first[112:], second[:16])
            return jnp.concatenate([first[:112], mixed, second[16:]], axis=0)
        def pair(t, i, q):
            phis, left = [], []
            for k in (2 * q, 2 * q + 1):
                if k < 8:
                    b = cid[k, t]
                    phis.append(hat_rows(ST, i, told[0, b], told[1, b], J))
                    left.append(rows_of(G[b], G[b + 128]))
                else:
                    b = fid[k - 8, t]
                    phis.append(hat_rows(ST, i, fdim[b], flev[b], J))
                    left.append(T[b])
            return jnp.concatenate(phis, axis=0), jnp.concatenate(left, axis=1)
        for q in (4, 5, 6, 7, 0, 1, 2, 3):
            m, stage = q % 2, (q // 2) % 2
            sums = accs if q < 4 else fines
            phi0, left0 = pair(t, i, q)
            phi1, left1 = pair(t + 1, i + 1, q)
            pltpu.matmul_push_rhs(jnp.concatenate([phi0, phi1], axis=1), stage, m)
            pltpu.matmul_acc_lhs(sums[m][0], left0, load_staged_rhs=stage)
            pltpu.matmul_acc_lhs(sums[m][1], left1)
            if q == 7:
                for n in range(2):
                    lanes = slice(128 * n, 128 * n + 128)
                    FS[ii % 2, n] = pltpu.matmul_pop(fines[0][n])[:120, lanes] + pltpu.matmul_pop(fines[1][n])[:120, lanes]
        for m in range(2):
            lane = lane0 + m * 128
            lanes = slice(128 * m, 128 * m + 128)
            here, there = part[i + m], FS[ii % 2, m]
            fine = jnp.concatenate([jnp.where(mine, here, there), jnp.where(mine, there, here)], axis=0)
            log = pltpu.matmul_pop(accs[0][m])[:, lanes] + pltpu.matmul_pop(accs[1][m])[:, lanes] + fine
            s = jnp.exp(log).astype(jnp.bfloat16)
            sav[:, :, pl.ds(lane, 128)] = s.reshape(60, 4, 128)
            total = jnp.sum(s.astype(jnp.float32).reshape(30, 8, 128), axis=0)
            cap[:, pl.ds(lane, 128)] = total[:4] + total[4:]
        return 0
    def scoped(*a):
        for ii in range(TPS // 2):
            tile((a[0:2], a[2:4]), (a[4:6], a[6:8]), ii, 0)
    pl.run_scoped(scoped, *(ACC(m, rows) for rows in (240, 128) for m in (0, 0, 1, 1)))
    W = TPS * 128
    capital = cap[...] * (1.0 / 60.0)
    sub = lax.broadcasted_iota(jnp.int32, (4, W), 0)
    tf = jnp.where(sub == 0, tfp[0], jnp.where(sub == 1, tfp[1], jnp.where(sub == 2, tfp[2], tfp[3])))
    logc = jnp.log(capital)
    interest = 0.33 * tf * jnp.exp(logc * (0.33 - 1.0)) + 1.0 - 0.1
    earnings = (1.0 - 0.33) * tf * jnp.exp(logc * 0.33)
    sh = jnp.concatenate([shock[pl.ds(step * TPS + i, 1), :] for i in range(TPS)], axis=1)
    w = jnp.zeros((4, W), jnp.float32)
    for k in range(4):
        col = jnp.where(sub == 0, tw[k, 0], jnp.where(sub == 1, tw[k, 1], jnp.where(sub == 2, tw[k, 2], tw[k, 3])))
        den = tw[k, 0] + tw[k, 1] + tw[k, 2] + tw[k, 3]
        w = jnp.where(sh == k, col / den, w)
    prices[0:1, :] = jnp.sum(w * interest, axis=0, keepdims=True)
    prices[1:2, :] = jnp.sum(w * earnings, axis=0, keepdims=True)

def evaluate(cid, fid, fdim, flev, tfp, tw, G, Fx, part, states, shock, g):
    n = states.shape[1]
    steps = n // (TPS * 128)
    smem = pl.BlockSpec(memory_space=pltpu.SMEM)
    vmem = pl.BlockSpec(memory_space=pltpu.VMEM)
    sav, prices = pl.pallas_call(
        eval_kernel,
        grid=(steps,),
        out_shape=(jax.ShapeDtypeStruct((60, 4, n), jnp.bfloat16), jax.ShapeDtypeStruct((2, n), jnp.float32)),
        in_specs=[smem] * 6 + [vmem] * 2 + [pl.BlockSpec((TPS, 120, 128), lambda i: (i, 0, 0)), pl.BlockSpec((59, TPS * 128), lambda i: (0, i)), vmem, smem],
        out_specs=(pl.BlockSpec((60, 4, TPS * 128), lambda i: (0, 0, i)), pl.BlockSpec((2, TPS * 128), lambda i: (0, i))),
        scratch_shapes=[pltpu.VMEM((32, 128, 128), jnp.bfloat16), pltpu.VMEM((4, TPS * 128), jnp.float32), pltpu.VMEM((TPS * 64, 128), jnp.float32), pltpu.VMEM((2, 2, 120, 128), jnp.float32), pltpu.VMEM((8, 128), jnp.int32), pltpu.SMEM((8, 128), jnp.int32), pltpu.SemaphoreType.DMA],
        compiler_params=pltpu.CompilerParams(vmem_limit_bytes=40 << 20),
        name="evaluate",
    )(*(stay(v) for v in (cid, fid, fdim, flev, tfp, tw)), G, Fx, part, stay(states), stay(shock), g)
    return sav, prices


def body(
    grid_states,
    coarse_active,
    fine_active,
    shock,
    coarse_surplus,
    fine_surplus,
    coarse_dim,
    coarse_level,
    fine_dim,
    fine_level,
    tfp,
    trans_weight,
):
    coarse = coarse_surplus.transpose(1, 0, 2).reshape(120, 128)
    rows = lax.broadcasted_iota(jnp.int32, (8, 128), 0)
    described = jnp.where(rows == 0, coarse_dim[0], coarse_level[0]).astype(jnp.bfloat16)
    piece = jnp.where(
        lax.axis_index("grp") == 0,
        jnp.concatenate([coarse, described], axis=0),
        jnp.concatenate([described, coarse], axis=0),
    )
    fine = fine_surplus.transpose(1, 0, 2)
    gathered, other, part = gather(piece, fine, fine_active.T, fine_dim, fine_level, grid_states)
    savings, prices = evaluate(
        coarse_active.T,
        fine_active.T,
        fine_dim,
        fine_level,
        tfp,
        trans_weight,
        gathered.reshape(256, 128, 128),
        other,
        part,
        grid_states,
        shock.reshape(-1, 128),
        lax.axis_index("grp").reshape(1).astype(jnp.int32),
    )
    return (savings.transpose(1, 0, 2), prices)


def solution(mesh):
    in_specs = (
        P(None, ("pts", "grp")),
        P(("pts", "grp"), None),
        P(("pts", "grp"), None),
        P(("pts", "grp")),
        P(None, "grp", "pts"),
        P(None, "grp", "pts"),
        P("pts"),
        P("pts"),
        P("pts"),
        P("pts"),
        P(),
        P(),
    )
    out_specs = (P(None, None, ("pts", "grp")), P(None, ("pts", "grp")))
    step = jax.shard_map(body, mesh=mesh, in_specs=in_specs, out_specs=out_specs, check_vma=False)

    def run(*args):
        with jax.sharding.use_abstract_mesh(mesh.abstract_mesh):
            return step(*args)

    return run
```

```python
import functools

import jax
import jax.numpy as jnp
from jax import lax
from jax.experimental import pallas as pl
from jax.experimental.pallas import tpu as pltpu
from jax.sharding import PartitionSpec as P

MESH = pl.DeviceIdType.MESH


def own_sums(fid, fdim, flev, fine, states, T, ST, part, quarter):
    def repack(k, _):
        T[k] = fine[:, :, pl.ds(pl.multiple_of(k * 128, 128), 128)].reshape(120, 128)
        return 0
    if quarter == 0:
        lax.fori_loop(0, fine.shape[2] // 128, repack, 0)
    J = basis()
    def tile(t, _):
        ST[pl.ds(0, 59), :] = states[:, pl.ds(pl.multiple_of(t * 128, 128), 128)]
        phis, left = [], []
        for k in range(8):
            b = fid[k, t]
            phis.append(hat_rows(ST, 0, fdim[b], flev[b], J))
            left.append(T[b])
        part[t] = jnp.dot(jnp.concatenate(left, axis=1), jnp.concatenate(phis, axis=0), preferred_element_type=jnp.float32)
        return 0
    size = part.shape[0] // 4
    lax.fori_loop(quarter * size, (quarter + 1) * size, tile, 0)


def basis():
    rows = lax.broadcasted_iota(jnp.int32, (16, 128), 0)
    return [(rows + 16 * q).astype(jnp.float32).astype(jnp.bfloat16) for q in range(8)]


def stay(v):
    return pltpu.with_memory_space_constraint(v, pltpu.HBM)


def gather_kernel(ids, dims, levels, piece, fine, states, G, F, part, zs, zr, xs, xr, ys, yr, ss, sr, fs, fr, ls, fine_v, states_v, T, ST, fid, fdim, flev, cs):
    p, g = lax.axis_index("pts"), lax.axis_index("grp")
    c, zl, x, y = p % 2, (p // 2) % 4, (p // 8) % 4, p // 32
    z = g * 4 + zl
    def dev(x, y, z, c):
        return {"pts": ((y * 4 + x) * 4 + z % 4) * 2 + c, "grp": z // 4}
    zd = lambda d: dev(x, y, (z + d + 8) % 8, c)
    xd = lambda d: dev((x + d + 4) % 4, y, z, c)
    yd = lambda d: dev(x, (y + d + 4) % 4, z, c)
    sib = dev(x, y, z, 1 - c)
    zo, xo = (4, 3, -3, 2, -2, 1, -1), (2, 1, -1)
    b = pltpu.get_barrier_semaphore()
    partners = [zd(d) for d in zo] + [xd(d) for d in xo] + [yd(d) for d in xo] + [sib]
    for d in partners:
        pl.semaphore_signal(b, 1, device_id=d, device_id_type=MESH)
    pl.semaphore_wait(b, len(partners))
    pend = []
    def rc(src, dst, s, r, d):
        cp = pltpu.make_async_remote_copy(src, dst, s, r, device_id=d, device_id_type=MESH)
        cp.start()
        pend.append(cp)
        return cp
    own = pltpu.make_async_copy(piece, G.at[g, y, x, zl, c], ls)
    zc = [rc(piece, G.at[g, y, x, zl, c], zs.at[i], zr.at[i], zd(d)) for i, d in enumerate(zo)]
    own.start()
    rc(fine, F, fs, fr, zd(4))
    pairs = ((fine, fine_v), (states, states_v), (ids, fid), (dims, fdim), (levels, flev))
    loads = [pltpu.make_async_copy(a, b, cs.at[i]) for i, (a, b) in enumerate(pairs)]
    for cp in loads: cp.start()
    for cp in loads: cp.wait()
    work = functools.partial(own_sums, fid, fdim, flev, fine_v, states_v, T, ST, part)
    work(0)
    own.wait()
    for cp in zc: cp.wait_recv()
    a = G.at[0, y, x, :, c]
    bb = G.at[1, y, x, :, c]
    s1 = []
    for i, d in enumerate(xo):
        s1.append(rc(a, a, xs.at[i], xr.at[i], xd(d)))
        s1.append(rc(bb, bb, ys.at[i], yr.at[i], yd(d)))
    work(1)
    for cp in s1: cp.wait_recv()
    def A(yy, z0=0, nz=4): return G.at[0, yy, :, pl.ds(z0, nz), c]
    def B(xx, z0=0, nz=4): return G.at[1, :, xx, pl.ds(z0, nz), c]
    def sibs(i, ref): rc(ref, ref, ss.at[i], sr.at[i], sib)
    ym, yp, xm, xp = (y + 3) % 4, (y + 1) % 4, (x + 3) % 4, (x + 1) % 4
    y2, x2 = (y + 2) % 4, (x + 2) % 4
    u = [rc(A(y), A(y), ys.at[3], yr.at[3], yd(1)), rc(B(x), B(x), xs.at[3], xr.at[3], xd(1)),
         rc(A(y), A(y), ys.at[4], yr.at[4], yd(-1)), rc(B(x), B(x), xs.at[4], xr.at[4], xd(-1))]
    sibs(0, A(y)); sibs(1, B(x))
    work(2)
    v = []
    u[0].wait_recv(); v.append(rc(A(ym, 0, 2), A(ym, 0, 2), ys.at[5], yr.at[5], yd(1))); sibs(2, A(ym))
    u[1].wait_recv(); v.append(rc(B(xm, 0, 2), B(xm, 0, 2), xs.at[5], xr.at[5], xd(1))); sibs(3, B(xm))
    u[2].wait_recv(); v.append(rc(A(yp, 2, 2), A(yp, 2, 2), ys.at[6], yr.at[6], yd(-1))); sibs(4, A(yp))
    u[3].wait_recv(); v.append(rc(B(xp, 2, 2), B(xp, 2, 2), xs.at[6], xr.at[6], xd(-1))); sibs(5, B(xp))
    work(3)
    for cp in v: cp.wait_recv()
    sibs(6, A(y2)); sibs(7, B(x2))
    done = set(id(q) for q in zc + s1 + u + v)
    for cp in pend:
        cp.wait_send()
        if id(cp) not in done: cp.wait_recv()

def gather(piece, fine, fid, fdim, flev, states):
    dma = pltpu.SemaphoreType.DMA
    tiles = states.shape[1] // 128
    return pl.pallas_call(
        gather_kernel,
        out_shape=(
            jax.ShapeDtypeStruct((2, 4, 4, 4, 2, 128, 128), jnp.bfloat16),
            jax.ShapeDtypeStruct(fine.shape, jnp.bfloat16),
            jax.ShapeDtypeStruct((tiles, 120, 128), jnp.float32),
        ),
        in_specs=[pl.BlockSpec(memory_space=pl.ANY)] * 6,
        out_specs=[pl.BlockSpec(memory_space=pltpu.VMEM)] * 3,
        scratch_shapes=[dma((7,)), dma((7,)), dma((7,)), dma((7,)), dma((7,)), dma((7,)), dma((8,)), dma((8,)), dma, dma, dma]
        + [pltpu.VMEM(fine.shape, jnp.bfloat16), pltpu.VMEM(states.shape, jnp.float32), pltpu.VMEM((32, 120, 128), jnp.bfloat16), pltpu.VMEM((64, 128), jnp.float32)]
        + [pltpu.SMEM(v.shape, jnp.int32) for v in (fid, fdim, flev)]
        + [dma((5,))],
        compiler_params=pltpu.CompilerParams(collective_id=0, has_side_effects=True, vmem_limit_bytes=24 << 20),
        name="gather",
    )(stay(fid), stay(fdim), stay(flev), piece, stay(fine), stay(states))


def ACC(m, rows):
    return pltpu.ACC(m)((rows, 256), jnp.float32)

TPS = 16

def hat_rows(states, lane0, dim, level, low_ref):
    row = jnp.broadcast_to(states[pl.ds(lane0 * 64 + dim, 1), :], (8, 128))
    scale = jnp.where(level == 0, 127.0, jnp.where(level == 1, 63.5, 31.75))
    scaled = row * scale
    lower = jnp.minimum(jnp.floor(scaled), 126.0)
    part = scaled - lower
    twice = lambda v: jnp.concatenate([v, v], axis=0).astype(jnp.bfloat16)
    lo = twice(1.0 - part)
    hi = twice(1.0 - jnp.abs(part - 1.0))
    at, nx = twice(lower), twice(lower + 1.0)
    out = []
    zero = jnp.zeros((16, 128), jnp.bfloat16)
    for q in range(8):
        j = low_ref[q]
        out.append(jnp.where(j == at, lo, jnp.where(j == nx, hi, zero)))
    return jnp.concatenate(out, axis=0)

def eval_kernel(cid, fid, fdim, flev, tfp, tw, G, Fx, part, states, shock, g_ref, sav, prices, T, cap, ST, FS, told_v, told, told_sem):
    step = pl.program_id(0)
    @pl.when(step == 0)
    def _():
        lane = lax.broadcasted_iota(jnp.int32, (8, 128), 1)
        said = jnp.zeros((8, 128), jnp.float32)
        for b in range(128):
            said = jnp.where(lane == b, G[b, pl.ds(120, 8), :].astype(jnp.float32), said)
        told_v[...] = said.astype(jnp.int32)
        telling = pltpu.make_async_copy(told_v, told, told_sem)
        telling.start()
        for k in range(32):
            T[k, pl.ds(0, 120), :] = Fx[:, :, pl.ds(128 * k, 128)].reshape(120, 128)
        telling.wait()
    for i in range(TPS):
        ST[pl.ds(64 * i, 59), :] = states[:, pl.ds(128 * i, 128)]
    J = basis()
    mine = g_ref[0] == 0

    def tile(accs, fines, ii, _):
        i = ii * 2
        t = step * TPS + i
        lane0 = i * 128
        upper = lax.broadcasted_iota(jnp.int32, (16, 128), 0) < 8
        def rows_of(first, second):
            mixed = jnp.where(upper, first[112:], second[:16])
            return jnp.concatenate([first[:112], mixed, second[16:]], axis=0)
        def pair(t, i, q):
            phis, left = [], []
            for k in (2 * q, 2 * q + 1):
                if k < 8:
                    b = cid[k, t]
                    phis.append(hat_rows(ST, i, told[0, b], told[1, b], J))
                    left.append(rows_of(G[b], G[b + 128]))
                else:
                    b = fid[k - 8, t]
                    phis.append(hat_rows(ST, i, fdim[b], flev[b], J))
                    left.append(T[b])
            return jnp.concatenate(phis, axis=0), jnp.concatenate(left, axis=1)
        for q in (4, 5, 6, 7, 0, 1, 2, 3):
            m, stage = q % 2, (q // 2) % 2
            sums = accs if q < 4 else fines
            phi0, left0 = pair(t, i, q)
            phi1, left1 = pair(t + 1, i + 1, q)
            pltpu.matmul_push_rhs(jnp.concatenate([phi0, phi1], axis=1), stage, m)
            pltpu.matmul_acc_lhs(sums[m][0], left0, load_staged_rhs=stage)
            pltpu.matmul_acc_lhs(sums[m][1], left1)
            if q == 7:
                for n in range(2):
                    lanes = slice(128 * n, 128 * n + 128)
                    FS[ii % 2, n] = pltpu.matmul_pop(fines[0][n])[:120, lanes] + pltpu.matmul_pop(fines[1][n])[:120, lanes]
        for m in range(2):
            lane = lane0 + m * 128
            lanes = slice(128 * m, 128 * m + 128)
            here, there = part[i + m], FS[ii % 2, m]
            fine = jnp.concatenate([jnp.where(mine, here, there), jnp.where(mine, there, here)], axis=0)
            log = pltpu.matmul_pop(accs[0][m])[:, lanes] + pltpu.matmul_pop(accs[1][m])[:, lanes] + fine
            s = jnp.exp(log).astype(jnp.bfloat16)
            sav[:, :, pl.ds(lane, 128)] = s.reshape(60, 4, 128)
            total = jnp.sum(s.astype(jnp.float32).reshape(30, 8, 128), axis=0)
            cap[:, pl.ds(lane, 128)] = total[:4] + total[4:]
        return 0
    def scoped(*a):
        for ii in range(TPS // 2):
            tile((a[0:2], a[2:4]), (a[4:6], a[6:8]), ii, 0)
    pl.run_scoped(scoped, *(ACC(m, rows) for rows in (240, 128) for m in (0, 0, 1, 1)))
    W = TPS * 128
    capital = cap[...] * (1.0 / 60.0)
    sub = lax.broadcasted_iota(jnp.int32, (4, W), 0)
    tf = jnp.where(sub == 0, tfp[0], jnp.where(sub == 1, tfp[1], jnp.where(sub == 2, tfp[2], tfp[3])))
    logc = jnp.log(capital)
    interest = 0.33 * tf * jnp.exp(logc * (0.33 - 1.0)) + 1.0 - 0.1
    earnings = (1.0 - 0.33) * tf * jnp.exp(logc * 0.33)
    sh = jnp.concatenate([shock[pl.ds(step * TPS + i, 1), :] for i in range(TPS)], axis=1)
    w = jnp.zeros((4, W), jnp.float32)
    for k in range(4):
        col = jnp.where(sub == 0, tw[k, 0], jnp.where(sub == 1, tw[k, 1], jnp.where(sub == 2, tw[k, 2], tw[k, 3])))
        den = tw[k, 0] + tw[k, 1] + tw[k, 2] + tw[k, 3]
        w = jnp.where(sh == k, col / den, w)
    prices[0:1, :] = jnp.sum(w * interest, axis=0, keepdims=True)
    prices[1:2, :] = jnp.sum(w * earnings, axis=0, keepdims=True)

def evaluate(cid, fid, fdim, flev, tfp, tw, G, Fx, part, states, shock, g):
    n = states.shape[1]
    steps = n // (TPS * 128)
    smem = pl.BlockSpec(memory_space=pltpu.SMEM)
    vmem = pl.BlockSpec(memory_space=pltpu.VMEM)
    sav, prices = pl.pallas_call(
        eval_kernel,
        grid=(steps,),
        out_shape=(jax.ShapeDtypeStruct((60, 4, n), jnp.bfloat16), jax.ShapeDtypeStruct((2, n), jnp.float32)),
        in_specs=[smem] * 6 + [vmem] * 2 + [pl.BlockSpec((TPS, 120, 128), lambda i: (i, 0, 0)), pl.BlockSpec((59, TPS * 128), lambda i: (0, i)), vmem, smem],
        out_specs=(pl.BlockSpec((60, 4, TPS * 128), lambda i: (0, 0, i)), pl.BlockSpec((2, TPS * 128), lambda i: (0, i))),
        scratch_shapes=[pltpu.VMEM((32, 128, 128), jnp.bfloat16), pltpu.VMEM((4, TPS * 128), jnp.float32), pltpu.VMEM((TPS * 64, 128), jnp.float32), pltpu.VMEM((2, 2, 120, 128), jnp.float32), pltpu.VMEM((8, 128), jnp.int32), pltpu.SMEM((8, 128), jnp.int32), pltpu.SemaphoreType.DMA],
        compiler_params=pltpu.CompilerParams(vmem_limit_bytes=40 << 20),
        name="evaluate",
    )(*(stay(v) for v in (cid, fid, fdim, flev, tfp, tw)), G, Fx, part, stay(states), stay(shock), g)
    return sav, prices


def body(
    grid_states,
    coarse_active,
    fine_active,
    shock,
    coarse_surplus,
    fine_surplus,
    coarse_dim,
    coarse_level,
    fine_dim,
    fine_level,
    tfp,
    trans_weight,
):
    coarse = coarse_surplus.transpose(1, 0, 2).reshape(120, 128)
    rows = lax.broadcasted_iota(jnp.int32, (8, 128), 0)
    described = jnp.where(rows == 0, coarse_dim[0], coarse_level[0]).astype(jnp.bfloat16)
    piece = jnp.where(
        lax.axis_index("grp") == 0,
        jnp.concatenate([coarse, described], axis=0),
        jnp.concatenate([described, coarse], axis=0),
    )
    fine = fine_surplus.transpose(1, 0, 2)
    gathered, other, part = gather(piece, fine, fine_active.T, fine_dim, fine_level, grid_states)
    savings, prices = evaluate(
        coarse_active.T,
        fine_active.T,
        fine_dim,
        fine_level,
        tfp,
        trans_weight,
        gathered.reshape(256, 128, 128),
        other,
        part,
        grid_states,
        shock.reshape(-1, 128),
        lax.axis_index("grp").reshape(1).astype(jnp.int32),
    )
    return (savings.transpose(1, 0, 2), prices)


def solution(mesh):
    in_specs = (
        P(None, ("pts", "grp")),
        P(("pts", "grp"), None),
        P(("pts", "grp"), None),
        P(("pts", "grp")),
        P(None, "grp", "pts"),
        P(None, "grp", "pts"),
        P("pts"),
        P("pts"),
        P("pts"),
        P("pts"),
        P(),
        P(),
    )
    out_specs = (P(None, None, ("pts", "grp")), P(None, ("pts", "grp")))
    step = jax.shard_map(body, mesh=mesh, in_specs=in_specs, out_specs=out_specs, check_vma=False)

    def run(*args):
        with jax.sharding.use_abstract_mesh(mesh.abstract_mesh):
            return step(*args)

    return run
```
